32 devices in a mesh: tm: 8 (over z, x), space: 4 (over y, core).
Axes of the slice: x: 2, y: 2, z: 4, core: 2. Of those that a mesh axis runs over, the one named last changes fastest.
Arguments:
- guess: float32 [8, 1, 64, 4096], P('tm', None, None, 'space'), may hold values from -6 to 6
- kernels: bfloat16 [16, 64, 576], P('tm'), may hold values from -0.25 to 0.25
- biases: float32 [16, 64], P('tm'), may hold values from -6 to 6
- probes: bfloat16 [2, 1, 64, 4096], P(None, None, None, 'space'), may hold values from -6 to 6
Outputs:
- states: float32 [8, 1, 64, 4096], P('tm', None, None, 'space')
- log_change: float32 [16], P('tm')
The draws below stay inside these ranges and needn't reach their ends.
All inputs are finite; a program needn't handle non-finite values.
Results may differ from the reference program's by a relative error of at most 0.0018.
Values may be sent and summed in bfloat16 or wider, within the bound.
A program may use at most 128 MiB of HBM per device.

```python
import jax
import jax.numpy as jnp
from jax import lax

CHANNELS = 64
WIDTH = 64
PROBES = 2
BATCH = 1
STEPS_DEV = 2
CELLS = 4096
GROUPS = 8
STEPS = 16
N_TM = 8


def block_levels(rng, extent, shards, least, top_value):
    factor_of = 1.0
    for dim, blocks in shards:
        steps = jax.random.uniform(jax.random.fold_in(jax.random.fold_in(rng, 6), dim), (blocks,), jnp.float32, least / len(shards), top_value / len(shards))
        factor_of = factor_of * jnp.repeat(jnp.exp(steps), extent[dim] // blocks).reshape((-1,) + (1,) * (len(extent) - 1 - dim))
    return factor_of


def normal_values(rng, extent, width, bound, shards=(), kind=jnp.bfloat16):
    result = width * jax.random.normal(rng, extent, jnp.float32)
    if shards:
        result = result * block_levels(rng, extent, shards, -0.22, 0.18)
    return jnp.clip(result, -bound, bound).astype(kind)


def setup_inputs(seed: int = 0) -> dict:
    key_list = jax.random.split(jax.random.key(seed), 5)
    return {
        "guess": normal_values(key_list[0], (GROUPS, BATCH, CHANNELS, CELLS), 1.0, 6.0, ((0, 8), (3, 4)), jnp.float32),
        "kernels": normal_values(key_list[1], (STEPS, CHANNELS, 9 * CHANNELS), (9 * CHANNELS) ** -0.5, 0.25, ((0, 8),)),
        "biases": normal_values(key_list[2], (STEPS, CHANNELS), 1.0, 6.0, ((0, 8),), jnp.float32),
        "probes": normal_values(key_list[3], (PROBES, BATCH, CHANNELS, CELLS), 1.0, 6.0, ((3, 4),)),
    }


step_size = 0.0078125


def gather_taps(stacked, row_len):
    out_rows = stacked.shape[2] // row_len - 2
    out_cells = out_rows * row_len
    padded = jnp.pad(stacked, ((0, 0), (0, 0), (1, 1)))
    column = jnp.arange(out_cells, dtype=jnp.int32) % row_len
    pieces = []
    for row_off in (-1, 0, 1):
        for col_off in (-1, 0, 1):
            offset = (1 + row_off) * row_len + col_off + 1
            window = padded[:, :, offset:offset + out_cells]
            if col_off == -1:
                window = jnp.where(column != 0, window, jnp.zeros_like(window))
            elif col_off == 1:
                window = jnp.where(column != row_len - 1, window, jnp.zeros_like(window))
            pieces.append(window)
    return jnp.concatenate(pieces, axis=1)


def advance(current, kernel, bias_row, probes):
    activation = jnp.tanh(current)
    slopes = 1.0 - activation * activation
    probe_vals = probes.astype(jnp.float32)
    inputs = jnp.concatenate([activation[None], slopes[None] * probe_vals], axis=0).astype(jnp.bfloat16)
    inputs = inputs.reshape((1 + PROBES) * BATCH, CHANNELS, CELLS)
    extended = jnp.pad(inputs, ((0, 0), (0, 0), (WIDTH, WIDTH)))
    stacked = gather_taps(extended, WIDTH)
    mixing = jnp.einsum("ok,skn->son", kernel.astype(jnp.float32), stacked.astype(jnp.float32), precision=lax.Precision.HIGHEST)
    forcing = mixing[:BATCH] + bias_row[None, :, None]
    probe_out = mixing[BATCH:].reshape(PROBES, BATCH, CHANNELS, CELLS)
    trace_value = jnp.sum(probe_vals * probe_out) / (PROBES * BATCH)
    return current + step_size * forcing, trace_value


def reference(guess, kernels, biases, probes):
    group_kernels = kernels.reshape(N_TM, STEPS_DEV, CHANNELS, 9 * CHANNELS)
    group_biases = biases.reshape(N_TM, STEPS_DEV, CHANNELS)

    def run_group(bundle):
        current, layer_kernels, layer_biases = bundle
        values = []
        for layer_index in range(STEPS_DEV):
            current, trace_value = advance(current, layer_kernels[layer_index], layer_biases[layer_index], probes)
            values.append(trace_value)
        return current, jnp.stack(values)

    finals, traces = lax.map(run_group, (guess, group_kernels, group_biases))
    summed = group_kernels.astype(jnp.float32).reshape(N_TM, STEPS_DEV, CHANNELS, 9, CHANNELS).sum(axis=(1, 3))
    coarse = jnp.eye(CHANNELS, dtype=jnp.float32)[None] + step_size * summed
    offsets = finals - jnp.einsum("kij,kbjn->kbin", coarse, guess, precision=lax.Precision.HIGHEST)

    def relay_step(carried, bundle):
        matrix, offset = bundle
        advanced = jnp.einsum("ij,bjn->bin", matrix, carried, precision=lax.Precision.HIGHEST) + offset
        return advanced, advanced

    final_state, remaining = lax.scan(relay_step, finals[0], (coarse[1:N_TM - 1], offsets[1:N_TM - 1]))
    states = jnp.concatenate([guess[0:1], finals[0:1], remaining], axis=0)
    log_change = -(step_size / WIDTH) * jnp.cumsum(traces.reshape(-1))
    return states, log_change
```

```python
import functools

import jax
import jax.numpy as jnp
from jax import lax
from jax.experimental import pallas as pl
from jax.experimental.pallas import tpu as pltpu
from jax.sharding import PartitionSpec as P

WIDTH = 64
LANES = 128
MESH = pl.DeviceIdType.MESH
step_size = 0.0078125
f32 = jnp.float32
bf16 = jnp.bfloat16


def split(value):
    high = value.astype(bf16)
    low = (value - high.astype(f32)).astype(bf16)
    return high, low


def exact_left(matrix):
    high, low = split(matrix)
    return jnp.concatenate([high.astype(f32), high.astype(f32), low.astype(f32)], axis=1).astype(bf16)


def exact_dot(left, field):
    high, low = split(field)
    return jnp.dot(left, jnp.concatenate([high, low, high], axis=0), preferred_element_type=f32)


def write_taps(target, base, first, count, value, column, row_len):
    width = value.shape[1]
    left = jnp.where(column != 0, pltpu.roll(value, 1, 1), 0.0)
    right = jnp.where(column != row_len - 1, pltpu.roll(value, width - 1, 1), 0.0)
    channels = value.shape[0]
    for dy in (-1, 0, 1):
        for index, source in enumerate((left, value, right)):
            tap = (dy + 1) * 3 + index
            moved = source if dy == 0 else pltpu.roll(source, (-dy * row_len) % width, 1)
            target[tap * channels:(tap + 1) * channels, base:base + count] = moved[:, first:first + count].astype(bf16)


def kernel(peers, strips, guess, kernels, biases, probes, states, logs,
           halo, probe_halo, stack, probe_stack, turned, mine, theirs, own_out, their_off,
           chain_in, chain_out, pass_out, trace_out, trace_in, pair_out, pair_in, run_out, run_in,
           halo_send, halo_recv, mat_sem, off_send, off_recv, chain_send, chain_recv,
           pass_send, pass_recv, trace_send, trace_recv, small_sem):
    row_len = WIDTH
    channels, cells = guess.shape[2], guess.shape[3]
    layers = kernels.shape[0]
    probe_count = probes.shape[0]
    taps = 9
    edge = layers * row_len
    wide = cells + 2 * edge
    rows = cells // row_len
    half = cells // 2
    chunks = half // LANES
    k = lax.axis_index("tm")
    s = lax.axis_index("space")
    q, x = k // 2, k % 2
    partner = q * 2 + 1 - x
    pairs = peers // 2

    def remote(src, dst, send, recv, tm, space):
        return pltpu.make_async_remote_copy(
            src_ref=src, dst_ref=dst, send_sem=send, recv_sem=recv, device_id=(tm, space), device_id_type=MESH)

    def chunk(side, c):
        return pl.ds(pl.multiple_of(side * half + c * LANES, LANES), LANES)

    barrier = pltpu.get_barrier_semaphore()
    for d in range(1, strips):
        pl.semaphore_signal(barrier, inc=1, device_id=(k, lax.rem(s + d, strips)), device_id_type=MESH)
    pl.semaphore_signal(barrier, inc=1, device_id=(partner, s), device_id_type=MESH)

    @pl.when(q > 0)
    def _():
        pl.semaphore_signal(barrier, inc=1, device_id=(k - 2, s), device_id_type=MESH)

    @pl.when(q < pairs - 1)
    def _():
        pl.semaphore_signal(barrier, inc=1, device_id=(k + 2, s), device_id_type=MESH)

    pl.semaphore_wait(barrier, strips + (q > 0).astype(jnp.int32) + (q < pairs - 1).astype(jnp.int32))

    up = remote(guess.at[0, 0, :, pl.ds(cells - edge, edge)], halo.at[0], halo_send.at[0], halo_recv.at[0], k, s + 1)
    down = remote(guess.at[0, 0, :, pl.ds(0, edge)], halo.at[1], halo_send.at[1], halo_recv.at[1], k, s - 1)
    probe_up = remote(probes.at[:, 0, :, pl.ds(cells - edge, edge)], probe_halo.at[0], halo_send.at[2], halo_recv.at[2], k, s + 1)
    probe_down = remote(probes.at[:, 0, :, pl.ds(0, edge)], probe_halo.at[1], halo_send.at[3], halo_recv.at[3], k, s - 1)
    has_up, has_down = s < strips - 1, s > 0

    @pl.when(has_up)
    def _():
        up.start()

    @pl.when(has_down)
    def _():
        down.start()

    @pl.when(has_up)
    def _():
        probe_up.start()

    @pl.when(has_down)
    def _():
        probe_down.start()

    first_pair = jnp.logical_and(q == 0, x == 0)
    seeds = [remote(guess.at[0, 0, :, pl.ds(half + c * LANES, LANES)], chain_in.at[c], pass_send.at[chunks + c], chain_recv.at[c], partner, s)
             for c in range(chunks)]

    @pl.when(first_pair)
    def _():
        for c in range(chunks):
            seeds[c].start()
        for c in range(chunks):
            chain_in[c] = guess[0, 0, :, c * LANES:(c + 1) * LANES]

    total = kernels[0].astype(f32)
    for n in range(1, layers):
        total = total + kernels[n].astype(f32)
    summed = total[:, 0:channels]
    for t in range(1, taps):
        summed = summed + total[:, t * channels:(t + 1) * channels]
    own_matrix = step_size * summed
    mine[:, 0:channels] = own_matrix
    mine[:, channels:2 * channels] = own_matrix
    mat = remote(mine, theirs, mat_sem.at[0], mat_sem.at[1], partner, s)
    mat.start()

    for n in range(layers):
        flipped = kernels[n].astype(f32)
        for t in range(taps):
            block = flipped[:, t * channels:(t + 1) * channels].T
            turned[n * channels:(n + 1) * channels, (taps - 1 - t) * channels:(taps - t) * channels] = block.astype(bf16)

    value = guess[0, 0]
    own_left = exact_left(own_matrix)
    mixed = exact_dot(own_left, value)

    position = lax.broadcasted_iota(jnp.int32, (1, wide), 1)
    column = position % row_len
    row = position // row_len - layers + s * rows
    inside = jnp.logical_and(row >= 0, row < rows * strips)
    diagonal = lax.broadcasted_iota(jnp.int32, (channels, channels), 0) == lax.broadcasted_iota(jnp.int32, (channels, channels), 1)

    @pl.when(has_down)
    def _():
        up.wait_recv()

    @pl.when(has_up)
    def _():
        down.wait_recv()

    current = jnp.concatenate([halo[0], value, halo[1]], axis=1)
    slopes = []
    for n in range(layers):
        activation = jnp.where(inside, jnp.tanh(current), 0.0)
        own = activation[:, edge:edge + cells]
        slopes.append(1.0 - own * own)
        last = n == layers - 1
        first, count = (edge, cells) if last else (0, wide)
        write_taps(stack, first, first, count, activation, column, row_len)
        forcing = jnp.dot(kernels[n], stack[:, first:first + count], preferred_element_type=f32)
        bias = jnp.sum(jnp.where(diagonal, biases[n:n + 1, :], 0.0), axis=1, keepdims=True)
        current = current[:, first:first + count] + step_size * (forcing + bias)
    own_out[...] = (current - value) - mixed

    offs = [remote(own_out.at[:, chunk(1 - x, c)], their_off.at[c], off_send.at[c], off_recv.at[c], partner, s)
            for c in range(chunks)]
    for c in range(chunks):
        offs[c].start()

    @pl.when(has_down)
    def _():
        probe_up.wait_recv()

    @pl.when(has_up)
    def _():
        probe_down.wait_recv()

    sums = [jnp.zeros((8, LANES), f32) for _ in range(layers)]
    for p in range(probe_count):
        field = probes[p, 0].astype(f32)
        padded = jnp.concatenate([probe_halo[0, p].astype(f32), field, probe_halo[1, p].astype(f32)], axis=1)
        padded = jnp.where(inside, padded, 0.0)
        write_taps(probe_stack, 0, edge, cells, padded, column, row_len)
        weights = jnp.dot(turned[...], probe_stack[...], preferred_element_type=f32)
        for n in range(layers):
            tangent = (slopes[n] * field).astype(bf16).astype(f32)
            product = tangent * weights[n * channels:(n + 1) * channels]
            part = product[:, 0:LANES]
            for c in range(1, cells // LANES):
                part = part + product[:, c * LANES:(c + 1) * LANES]
            for r in range(channels // 8):
                sums[n] = sums[n] + part[r * 8:(r + 1) * 8]
    for n in range(layers):
        trace_out[n * 8:(n + 1) * 8] = sums[n]
    traces = [remote(trace_out, trace_in.at[d - 1], trace_send.at[d - 1], trace_recv.at[d - 1], k, lax.rem(s + d, strips))
              for d in range(1, strips)]
    for copy in traces:
        copy.start()

    mat.wait_recv()
    other_matrix = theirs[:, 0:channels]
    even = x == 0
    early = jnp.where(even, own_matrix, other_matrix)
    late = jnp.where(even, other_matrix, own_matrix)
    late_left = exact_left(late)
    both = early + late + exact_dot(late_left, early)
    map_left = exact_left(jnp.concatenate([both, early], axis=0))

    nexts = [remote(chain_out.at[c], chain_in.at[c], chain_send.at[c], chain_recv.at[c], k + 2, s) for c in range(chunks)]
    passes = [remote(pass_out.at[c], states.at[0, 0, :, chunk(x, c)], pass_send.at[c], pass_recv.at[c], partner, s)
              for c in range(chunks)]
    passed = [remote(pass_out.at[c], states.at[0, 0, :, chunk(1 - x, c)], pass_send.at[c], pass_recv.at[c], partner, s)
              for c in range(chunks)]
    pair = remote(pair_out, pair_in, small_sem.at[0], small_sem.at[1], partner, s)
    onward = remote(run_out, run_in, small_sem.at[2], small_sem.at[3], k + 2, s)
    go_on = q < pairs - 1
    waits = jnp.logical_not(first_pair)
    early_offs, sum_offs = [], []
    for c in range(chunks):
        offs[c].wait_recv()
        held = own_out[:, chunk(x, c)]
        got = their_off[c]
        early_off = jnp.where(even, held, got)
        late_off = jnp.where(even, got, held)
        early_offs.append(early_off)
        sum_offs.append(late_off + early_off + exact_dot(late_left, early_off))
    for c in range(chunks):
        @pl.when(waits)
        def _():
            nexts[c].wait_recv()

        here = chain_in[c]
        moved = exact_dot(map_left, here)
        chain_out[c] = here + (moved[0:channels] + sum_offs[c])

        @pl.when(go_on)
        def _():
            nexts[c].start()

        between = here + (moved[channels:2 * channels] + early_offs[c])
        pass_out[c] = jnp.where(even, between, here)
        passes[c].start()
        states[0, 0, :, chunk(x, c)] = jnp.where(even, here, between)
        if c == max(chunks - 2, 0):
            trace_total = trace_out[...]
            for copy in traces:
                copy.wait_recv()
            for d in range(1, strips):
                trace_total = trace_total + trace_in[d - 1]
            pair_out[...] = trace_total
            pair.start()

    pair.wait_recv()

    def layer_sum(tile):
        result = tile[0:8]
        for n in range(1, layers):
            result = result + tile[n * 8:(n + 1) * 8]
        return result

    own_sum, pair_sum = layer_sum(trace_total), layer_sum(pair_in[...])

    @pl.when(q == 0)
    def _():
        run_in[...] = jnp.zeros_like(run_in)

    @pl.when(q > 0)
    def _():
        onward.wait_recv()

    running = run_in[...]
    run_out[...] = running + own_sum + pair_sum

    @pl.when(go_on)
    def _():
        onward.start()

    running = running + jnp.where(even, 0.0, pair_sum)
    for n in range(layers):
        running = running + trace_total[n * 8:(n + 1) * 8]
        logs[n] = jnp.sum(running) * (-(step_size / row_len) / probe_count)

    for c in range(chunks):
        passed[c].wait_recv()
    for c in range(chunks):
        passes[c].wait_send()
        offs[c].wait_send()
    for copy in traces:
        copy.wait_send()
    mat.wait_send()
    pair.wait_send()

    @pl.when(go_on)
    def _():
        for c in range(chunks):
            nexts[c].wait_send()
        onward.wait_send()

    @pl.when(first_pair)
    def _():
        for c in range(chunks):
            seeds[c].wait_send()

    @pl.when(has_up)
    def _():
        up.wait_send()
        probe_up.wait_send()

    @pl.when(has_down)
    def _():
        down.wait_send()
        probe_down.wait_send()


def solution(mesh):
    peers, strips = mesh.shape["tm"], mesh.shape["space"]

    def step(guess, kernels, biases, probes):
        channels, cells = guess.shape[2], guess.shape[3]
        layers = kernels.shape[0]
        probe_count = probes.shape[0]
        edge = layers * WIDTH
        chunks = cells // 2 // LANES
        depth = kernels.shape[2]
        dma = pltpu.SemaphoreType.DMA
        tile = (chunks, channels, LANES)
        return pl.pallas_call(
            functools.partial(kernel, peers, strips),
            out_shape=(
                jax.ShapeDtypeStruct(guess.shape, f32),
                jax.ShapeDtypeStruct((layers,), f32),
            ),
            in_specs=[pl.BlockSpec(memory_space=pltpu.VMEM)] * 4,
            out_specs=(pl.BlockSpec(memory_space=pltpu.VMEM), pl.BlockSpec(memory_space=pltpu.SMEM)),
            scratch_shapes=[
                pltpu.VMEM((2, channels, edge), f32),
                pltpu.VMEM((2, probe_count, channels, edge), bf16),
                pltpu.VMEM((depth, cells + 2 * edge), bf16),
                pltpu.VMEM((depth, cells), bf16),
                pltpu.VMEM((layers * channels, depth), bf16),
                pltpu.VMEM((channels, 2 * channels), f32),
                pltpu.VMEM((channels, 2 * channels), f32),
                pltpu.VMEM((channels, cells), f32),
                pltpu.VMEM(tile, f32),
                pltpu.VMEM(tile, f32),
                pltpu.VMEM(tile, f32),
                pltpu.VMEM(tile, f32),
                pltpu.VMEM((layers * 8, LANES), f32),
                pltpu.VMEM((max(strips - 1, 1), layers * 8, LANES), f32),
                pltpu.VMEM((layers * 8, LANES), f32),
                pltpu.VMEM((layers * 8, LANES), f32),
                pltpu.VMEM((8, LANES), f32),
                pltpu.VMEM((8, LANES), f32),
                dma((4,)), dma((4,)), dma((2,)), dma((chunks,)), dma((chunks,)), dma((chunks,)), dma((chunks,)),
                dma((2 * chunks,)), dma((chunks,)), dma((max(strips - 1, 1),)), dma((max(strips - 1, 1),)), dma((4,)),
            ],
            compiler_params=pltpu.CompilerParams(collective_id=0, has_side_effects=True),
        )(guess, kernels, biases, probes)

    return jax.shard_map(
        step,
        mesh=mesh,
        in_specs=(
            P("tm", None, None, "space"),
            P("tm", None, None),
            P("tm", None),
            P(None, None, None, "space"),
        ),
        out_specs=(P("tm", None, None, "space"), P("tm")),
        check_vma=False,
    )
```

```python
import functools

import jax
import jax.numpy as jnp
from jax import lax
from jax.experimental import pallas as pl
from jax.experimental.pallas import tpu as pltpu
from jax.sharding import PartitionSpec as P

WIDTH = 64
LANES = 128
MESH = pl.DeviceIdType.MESH
step_size = 0.0078125
f32 = jnp.float32
bf16 = jnp.bfloat16


def split(value):
    high = value.astype(bf16)
    low = (value - high.astype(f32)).astype(bf16)
    return high, low


def exact_left(matrix):
    high, low = split(matrix)
    return jnp.concatenate([high.astype(f32), high.astype(f32), low.astype(f32)], axis=1).astype(bf16)


def exact_dot(left, field):
    high, low = split(field)
    return jnp.dot(left, jnp.concatenate([high, low, high], axis=0), preferred_element_type=f32)


def write_taps(target, base, first, count, value, column, row_len):
    width = value.shape[1]
    left = jnp.where(column != 0, pltpu.roll(value, 1, 1), 0.0)
    right = jnp.where(column != row_len - 1, pltpu.roll(value, width - 1, 1), 0.0)
    channels = value.shape[0]
    for dy in (-1, 0, 1):
        for index, source in enumerate((left, value, right)):
            tap = (dy + 1) * 3 + index
            moved = source if dy == 0 else pltpu.roll(source, (-dy * row_len) % width, 1)
            target[tap * channels:(tap + 1) * channels, base:base + count] = moved[:, first:first + count].astype(bf16)


def kernel(peers, strips, guess_in, kernels_in, biases_in, probes_in, states, logs,
           guess, kernels, biases, probes, load_sem, halo, probe_halo, stack, probe_stack, turned, mine, theirs, own_out, their_off,
           chain_in, chain_out, pass_out, trace_out, trace_in, pair_out, pair_in, run_out, run_in,
           halo_send, halo_recv, mat_sem, off_send, off_recv, chain_send, chain_recv,
           pass_send, pass_recv, trace_send, trace_recv, small_sem):
    row_len = WIDTH
    channels, cells = guess.shape[2], guess.shape[3]
    layers = kernels.shape[0]
    probe_count = probes.shape[0]
    taps = 9
    edge = layers * row_len
    wide = cells + 2 * edge
    rows = cells // row_len
    half = cells // 2
    chunks = half // LANES
    k = lax.axis_index("tm")
    s = lax.axis_index("space")
    q, x = k // 2, k % 2
    partner = q * 2 + 1 - x
    pairs = peers // 2

    def remote(src, dst, send, recv, tm, space):
        return pltpu.make_async_remote_copy(
            src_ref=src, dst_ref=dst, send_sem=send, recv_sem=recv, device_id=(tm, space), device_id_type=MESH)

    def chunk(side, c):
        return pl.ds(pl.multiple_of(side * half + c * LANES, LANES), LANES)

    loads = [pltpu.make_async_copy(src, dst, load_sem.at[i]) for i, (src, dst) in enumerate(
        ((kernels_in, kernels), (guess_in, guess), (biases_in, biases), (probes_in, probes)))]
    for load in loads:
        load.start()

    barrier = pltpu.get_barrier_semaphore()
    for d in range(1, strips):
        pl.semaphore_signal(barrier, inc=1, device_id=(k, lax.rem(s + d, strips)), device_id_type=MESH)
    pl.semaphore_signal(barrier, inc=1, device_id=(partner, s), device_id_type=MESH)

    @pl.when(q > 0)
    def _():
        pl.semaphore_signal(barrier, inc=1, device_id=(k - 2, s), device_id_type=MESH)

    @pl.when(q < pairs - 1)
    def _():
        pl.semaphore_signal(barrier, inc=1, device_id=(k + 2, s), device_id_type=MESH)

    pl.semaphore_wait(barrier, strips + (q > 0).astype(jnp.int32) + (q < pairs - 1).astype(jnp.int32))

    up = remote(guess_in.at[0, 0, :, pl.ds(cells - edge, edge)], halo.at[0], halo_send.at[0], halo_recv.at[0], k, s + 1)
    down = remote(guess_in.at[0, 0, :, pl.ds(0, edge)], halo.at[1], halo_send.at[1], halo_recv.at[1], k, s - 1)
    probe_up = remote(probes_in.at[:, 0, :, pl.ds(cells - edge, edge)], probe_halo.at[0], halo_send.at[2], halo_recv.at[2], k, s + 1)
    probe_down = remote(probes_in.at[:, 0, :, pl.ds(0, edge)], probe_halo.at[1], halo_send.at[3], halo_recv.at[3], k, s - 1)
    has_up, has_down = s < strips - 1, s > 0

    @pl.when(has_up)
    def _():
        up.start()

    @pl.when(has_down)
    def _():
        down.start()

    @pl.when(has_up)
    def _():
        probe_up.start()

    @pl.when(has_down)
    def _():
        probe_down.start()

    first_pair = jnp.logical_and(q == 0, x == 0)
    seeds = [remote(guess_in.at[0, 0, :, pl.ds(half + c * LANES, LANES)], chain_in.at[c], pass_send.at[chunks + c], chain_recv.at[c], partner, s)
             for c in range(chunks)]

    @pl.when(first_pair)
    def _():
        for c in range(chunks):
            seeds[c].start()

    for load in loads:
        load.wait()

    @pl.when(first_pair)
    def _():
        for c in range(chunks):
            chain_in[c] = guess[0, 0, :, c * LANES:(c + 1) * LANES]

    total = kernels[0].astype(f32)
    for n in range(1, layers):
        total = total + kernels[n].astype(f32)
    summed = total[:, 0:channels]
    for t in range(1, taps):
        summed = summed + total[:, t * channels:(t + 1) * channels]
    own_matrix = step_size * summed
    mine[:, 0:channels] = own_matrix
    mine[:, channels:2 * channels] = own_matrix
    mat = remote(mine, theirs, mat_sem.at[0], mat_sem.at[1], partner, s)
    mat.start()

    for n in range(layers):
        flipped = kernels[n].astype(f32)
        for t in range(taps):
            block = flipped[:, t * channels:(t + 1) * channels].T
            turned[n * channels:(n + 1) * channels, (taps - 1 - t) * channels:(taps - t) * channels] = block.astype(bf16)

    value = guess[0, 0]
    own_left = exact_left(own_matrix)
    mixed = exact_dot(own_left, value)

    position = lax.broadcasted_iota(jnp.int32, (1, wide), 1)
    column = position % row_len
    row = position // row_len - layers + s * rows
    inside = jnp.logical_and(row >= 0, row < rows * strips)
    diagonal = lax.broadcasted_iota(jnp.int32, (channels, channels), 0) == lax.broadcasted_iota(jnp.int32, (channels, channels), 1)

    @pl.when(has_down)
    def _():
        up.wait_recv()

    @pl.when(has_up)
    def _():
        down.wait_recv()

    current = jnp.concatenate([halo[0], value, halo[1]], axis=1)
    slopes = []
    for n in range(layers):
        activation = jnp.where(inside, jnp.tanh(current), 0.0)
        own = activation[:, edge:edge + cells]
        slopes.append(1.0 - own * own)
        last = n == layers - 1
        first, count = (edge, cells) if last else (0, wide)
        write_taps(stack, first, first, count, activation, column, row_len)
        forcing = jnp.dot(kernels[n], stack[:, first:first + count], preferred_element_type=f32)
        bias = jnp.sum(jnp.where(diagonal, biases[n:n + 1, :], 0.0), axis=1, keepdims=True)
        current = current[:, first:first + count] + step_size * (forcing + bias)
    own_out[...] = (current - value) - mixed

    offs = [remote(own_out.at[:, chunk(1 - x, c)], their_off.at[c], off_send.at[c], off_recv.at[c], partner, s)
            for c in range(chunks)]
    for c in range(chunks):
        offs[c].start()

    @pl.when(has_down)
    def _():
        probe_up.wait_recv()

    @pl.when(has_up)
    def _():
        probe_down.wait_recv()

    sums = [jnp.zeros((8, LANES), f32) for _ in range(layers)]
    for p in range(probe_count):
        field = probes[p, 0].astype(f32)
        padded = jnp.concatenate([probe_halo[0, p].astype(f32), field, probe_halo[1, p].astype(f32)], axis=1)
        padded = jnp.where(inside, padded, 0.0)
        write_taps(probe_stack, 0, edge, cells, padded, column, row_len)
        weights = jnp.dot(turned[...], probe_stack[...], preferred_element_type=f32)
        for n in range(layers):
            tangent = (slopes[n] * field).astype(bf16).astype(f32)
            product = tangent * weights[n * channels:(n + 1) * channels]
            part = product[:, 0:LANES]
            for c in range(1, cells // LANES):
                part = part + product[:, c * LANES:(c + 1) * LANES]
            for r in range(channels // 8):
                sums[n] = sums[n] + part[r * 8:(r + 1) * 8]
    for n in range(layers):
        trace_out[n * 8:(n + 1) * 8] = sums[n]
    traces = [remote(trace_out, trace_in.at[d - 1], trace_send.at[d - 1], trace_recv.at[d - 1], k, lax.rem(s + d, strips))
              for d in range(1, strips)]
    for copy in traces:
        copy.start()

    mat.wait_recv()
    other_matrix = theirs[:, 0:channels]
    even = x == 0
    early = jnp.where(even, own_matrix, other_matrix)
    late = jnp.where(even, other_matrix, own_matrix)
    late_left = exact_left(late)
    both = early + late + exact_dot(late_left, early)
    map_left = exact_left(jnp.concatenate([both, early], axis=0))

    nexts = [remote(chain_out.at[c], chain_in.at[c], chain_send.at[c], chain_recv.at[c], k + 2, s) for c in range(chunks)]
    passes = [remote(pass_out.at[c], states.at[0, 0, :, chunk(x, c)], pass_send.at[c], pass_recv.at[c], partner, s)
              for c in range(chunks)]
    passed = [remote(pass_out.at[c], states.at[0, 0, :, chunk(1 - x, c)], pass_send.at[c], pass_recv.at[c], partner, s)
              for c in range(chunks)]
    pair = remote(pair_out, pair_in, small_sem.at[0], small_sem.at[1], partner, s)
    onward = remote(run_out, run_in, small_sem.at[2], small_sem.at[3], k + 2, s)
    go_on = q < pairs - 1
    waits = jnp.logical_not(first_pair)
    for c in range(chunks):
        offs[c].wait_recv()
        held = own_out[:, chunk(x, c)]
        got = their_off[c]
        early_off = jnp.where(even, held, got)
        late_off = jnp.where(even, got, held)
        sum_off = late_off + early_off + exact_dot(late_left, early_off)

        @pl.when(waits)
        def _():
            nexts[c].wait_recv()

        here = chain_in[c]
        moved = exact_dot(map_left, here)
        chain_out[c] = here + (moved[0:channels] + sum_off)

        @pl.when(go_on)
        def _():
            nexts[c].start()

        between = here + (moved[channels:2 * channels] + early_off)
        pass_out[c] = jnp.where(even, between, here)
        passes[c].start()
        states[0, 0, :, chunk(x, c)] = jnp.where(even, here, between)
        if c == max(chunks - 2, 0):
            trace_total = trace_out[...]
            for copy in traces:
                copy.wait_recv()
            for d in range(1, strips):
                trace_total = trace_total + trace_in[d - 1]
            pair_out[...] = trace_total
            pair.start()

    pair.wait_recv()

    def layer_sum(tile):
        result = tile[0:8]
        for n in range(1, layers):
            result = result + tile[n * 8:(n + 1) * 8]
        return result

    own_sum, pair_sum = layer_sum(trace_total), layer_sum(pair_in[...])

    @pl.when(q == 0)
    def _():
        run_in[...] = jnp.zeros_like(run_in)

    @pl.when(q > 0)
    def _():
        onward.wait_recv()

    running = run_in[...]
    run_out[...] = running + own_sum + pair_sum

    @pl.when(go_on)
    def _():
        onward.start()

    running = running + jnp.where(even, 0.0, pair_sum)
    for n in range(layers):
        running = running + trace_total[n * 8:(n + 1) * 8]
        logs[n * 8:(n + 1) * 8] = running * (-(step_size / row_len) / probe_count)

    for c in range(chunks):
        passed[c].wait_recv()
    for c in range(chunks):
        passes[c].wait_send()
        offs[c].wait_send()
    for copy in traces:
        copy.wait_send()
    mat.wait_send()
    pair.wait_send()

    @pl.when(go_on)
    def _():
        for c in range(chunks):
            nexts[c].wait_send()
        onward.wait_send()

    @pl.when(first_pair)
    def _():
        for c in range(chunks):
            seeds[c].wait_send()

    @pl.when(has_up)
    def _():
        up.wait_send()
        probe_up.wait_send()

    @pl.when(has_down)
    def _():
        down.wait_send()
        probe_down.wait_send()


def finish(states_in, tiles, states, logs, sem):
    copy = pltpu.make_async_copy(states_in, states, sem)
    copy.start()
    for n in range(logs.shape[0]):
        logs[n] = jnp.sum(tiles[n * 8:(n + 1) * 8])
    copy.wait()


def solution(mesh):
    peers, strips = mesh.shape["tm"], mesh.shape["space"]

    def step(guess, kernels, biases, probes):
        channels, cells = guess.shape[2], guess.shape[3]
        layers = kernels.shape[0]
        probe_count = probes.shape[0]
        edge = layers * WIDTH
        chunks = cells // 2 // LANES
        depth = kernels.shape[2]
        dma = pltpu.SemaphoreType.DMA
        tile = (chunks, channels, LANES)
        states, tiles = pl.pallas_call(
            functools.partial(kernel, peers, strips),
            out_shape=(
                pltpu.VMEM(guess.shape, f32),
                pltpu.VMEM((layers * 8, LANES), f32),
            ),
            in_specs=[pl.BlockSpec(memory_space=pl.ANY)] * 4,
            out_specs=(pl.BlockSpec(memory_space=pltpu.VMEM), pl.BlockSpec(memory_space=pltpu.VMEM)),
            scratch_shapes=[
                pltpu.VMEM(guess.shape, guess.dtype),
                pltpu.VMEM(kernels.shape, kernels.dtype),
                pltpu.VMEM(biases.shape, biases.dtype),
                pltpu.VMEM(probes.shape, probes.dtype),
                dma((4,)),
                pltpu.VMEM((2, channels, edge), f32),
                pltpu.VMEM((2, probe_count, channels, edge), bf16),
                pltpu.VMEM((depth, cells + 2 * edge), bf16),
                pltpu.VMEM((depth, cells), bf16),
                pltpu.VMEM((layers * channels, depth), bf16),
                pltpu.VMEM((channels, 2 * channels), f32),
                pltpu.VMEM((channels, 2 * channels), f32),
                pltpu.VMEM((channels, cells), f32),
                pltpu.VMEM(tile, f32),
                pltpu.VMEM(tile, f32),
                pltpu.VMEM(tile, f32),
                pltpu.VMEM(tile, f32),
                pltpu.VMEM((layers * 8, LANES), f32),
                pltpu.VMEM((max(strips - 1, 1), layers * 8, LANES), f32),
                pltpu.VMEM((layers * 8, LANES), f32),
                pltpu.VMEM((layers * 8, LANES), f32),
                pltpu.VMEM((8, LANES), f32),
                pltpu.VMEM((8, LANES), f32),
                dma((4,)), dma((4,)), dma((2,)), dma((chunks,)), dma((chunks,)), dma((chunks,)), dma((chunks,)),
                dma((2 * chunks,)), dma((chunks,)), dma((max(strips - 1, 1),)), dma((max(strips - 1, 1),)), dma((4,)),
            ],
            compiler_params=pltpu.CompilerParams(collective_id=0, has_side_effects=True),
        )(guess, kernels, biases, probes)
        return pl.pallas_call(
            finish,
            out_shape=(
                jax.ShapeDtypeStruct(guess.shape, f32),
                jax.ShapeDtypeStruct((layers,), f32),
            ),
            in_specs=[pl.BlockSpec(memory_space=pltpu.VMEM)] * 2,
            out_specs=(pl.BlockSpec(memory_space=pl.ANY), pl.BlockSpec(memory_space=pltpu.SMEM)),
            scratch_shapes=[dma],
        )(pltpu.with_memory_space_constraint(states, pltpu.VMEM), pltpu.with_memory_space_constraint(tiles, pltpu.VMEM))

    return jax.shard_map(
        step,
        mesh=mesh,
        in_specs=(
            P("tm", None, None, "space"),
            P("tm", None, None),
            P("tm", None),
            P(None, None, None, "space"),
        ),
        out_specs=(P("tm", None, None, "space"), P("tm")),
        check_vma=False,
    )
```

```python
import functools

import jax
import jax.numpy as jnp
from jax import lax
from jax.experimental import pallas as pl
from jax.experimental.pallas import tpu as pltpu
from jax.sharding import PartitionSpec as P

WIDTH = 64
LANES = 128
MESH = pl.DeviceIdType.MESH
step_size = 0.0078125
f32 = jnp.float32
bf16 = jnp.bfloat16


def split(value):
    high = value.astype(bf16)
    low = (value - high.astype(f32)).astype(bf16)
    return high, low


def exact_left(matrix):
    high, low = split(matrix)
    return jnp.concatenate([high.astype(f32), high.astype(f32), low.astype(f32)], axis=1).astype(bf16)


def exact_dot(left, field):
    high, low = split(field)
    return jnp.dot(left, jnp.concatenate([high, low, high], axis=0), preferred_element_type=f32)


def write_taps(target, base, first, count, value, column, row_len):
    width = value.shape[1]
    left = jnp.where(column != 0, pltpu.roll(value, 1, 1), 0.0)
    right = jnp.where(column != row_len - 1, pltpu.roll(value, width - 1, 1), 0.0)
    channels = value.shape[0]
    for dy in (-1, 0, 1):
        for index, source in enumerate((left, value, right)):
            tap = (dy + 1) * 3 + index
            moved = source if dy == 0 else pltpu.roll(source, (-dy * row_len) % width, 1)
            target[tap * channels:(tap + 1) * channels, base:base + count] = moved[:, first:first + count].astype(bf16)


def kernel(peers, strips, guess_in, kernels_in, biases_in, probes_in, states, logs,
           window, kernels, biases, probes, stack, probe_stack, turned, offsets, slopes, sum_offs,
           chain_in, chain_out, pass_out, trace_out, trace_in, run_out, run_in,
           load_sem, edge_send, edge_recv, swap_send, swap_recv, chain_send, chain_recv,
           pass_send, pass_recv, trace_send, trace_recv, run_sem):
    row_len = WIDTH
    channels, cells = guess_in.shape[2], guess_in.shape[3]
    layers = kernels_in.shape[0]
    probe_count = probes_in.shape[0]
    taps = 9
    edge = layers * row_len
    rows = cells // row_len
    half = cells // 2
    part = half + edge
    wide = half + 2 * edge
    chunks = half // LANES
    k = lax.axis_index("tm")
    s = lax.axis_index("space")
    q, x = k // 2, k % 2
    other = 1 - x
    partner = q * 2 + other
    pairs = peers // 2
    even = x == 0

    def remote(src, dst, send, recv, tm, space):
        return pltpu.make_async_remote_copy(
            src_ref=src, dst_ref=dst, send_sem=send, recv_sem=recv, device_id=(tm, space), device_id_type=MESH)

    def chunk(side, c):
        return pl.ds(pl.multiple_of(side * half + c * LANES, LANES), LANES)

    def aligned(start, size):
        return pl.ds(pl.multiple_of(start, LANES), size)

    mine = aligned(x * (half - edge), part)
    place = aligned(other * edge, part)
    loads = [pltpu.make_async_copy(src, dst, load_sem.at[i]) for i, (src, dst) in enumerate((
        (guess_in.at[0, 0, :, mine], window.at[x, :, place]),
        (kernels_in, kernels.at[x]),
        (biases_in, biases.at[x]),
        (probes_in.at[:, 0, :, mine], probes.at[:, :, place])))]
    for load in loads:
        load.start()

    barrier = pltpu.get_barrier_semaphore()
    spot = x * strips + s
    ring = []
    for d in range(1, 2 * strips):
        to = lax.rem(spot + d, 2 * strips)
        ring.append((q * 2 + to // strips, lax.rem(to, strips)))
    for tm, space in ring:
        pl.semaphore_signal(barrier, inc=1, device_id=(tm, space), device_id_type=MESH)

    @pl.when(q > 0)
    def _():
        pl.semaphore_signal(barrier, inc=1, device_id=(k - 2, s), device_id_type=MESH)

    @pl.when(q < pairs - 1)
    def _():
        pl.semaphore_signal(barrier, inc=1, device_id=(k + 2, s), device_id_type=MESH)

    pl.semaphore_wait(barrier, 2 * strips - 1 + (q > 0).astype(jnp.int32) + (q < pairs - 1).astype(jnp.int32))

    has_up, has_down = s < strips - 1, s > 0
    last_rows, first_rows = pl.ds(cells - edge, edge), pl.ds(0, edge)
    up = remote(guess_in.at[0, 0, :, last_rows], window.at[x, :, pl.ds(0, edge)], edge_send.at[0], edge_recv.at[x], q * 2, s + 1)
    down = remote(guess_in.at[0, 0, :, first_rows], window.at[x, :, pl.ds(part, edge)], edge_send.at[1], edge_recv.at[x], q * 2 + 1, s - 1)
    probe_up = remote(probes_in.at[:, 0, :, last_rows], probes.at[:, :, pl.ds(0, edge)], edge_send.at[2], edge_recv.at[2], k, s + 1)
    probe_down = remote(probes_in.at[:, 0, :, first_rows], probes.at[:, :, pl.ds(part, edge)], edge_send.at[2], edge_recv.at[2], k, s - 1)
    theirs = aligned(other * (half - edge), part)
    swaps = [
        remote(guess_in.at[0, 0, :, theirs], window.at[x, :, aligned(x * edge, part)], swap_send.at[0], swap_recv.at[0], partner, s),
        remote(kernels_in, kernels.at[x], swap_send.at[1], swap_recv.at[1], partner, s),
        remote(biases_in, biases.at[x], swap_send.at[2], swap_recv.at[2], partner, s),
    ]
    send_probe_up = jnp.logical_and(even, has_up)
    send_probe_down = jnp.logical_and(x == 1, has_down)

    @pl.when(has_up)
    def _():
        up.start()

    @pl.when(has_down)
    def _():
        down.start()

    for i in (1, 0, 2):
        swaps[i].start()

    @pl.when(send_probe_up)
    def _():
        probe_up.start()

    @pl.when(send_probe_down)
    def _():
        probe_down.start()

    def wait_edge(group):
        left = remote(guess_in.at[0, 0, :, last_rows], window.at[group, :, pl.ds(0, edge)], edge_send.at[0], edge_recv.at[group], k, s)
        right = remote(guess_in.at[0, 0, :, first_rows], window.at[group, :, pl.ds(part, edge)], edge_send.at[1], edge_recv.at[group], k, s)

        @pl.when(jnp.logical_and(even, has_down))
        def _():
            left.wait_recv()

        @pl.when(jnp.logical_and(x == 1, has_up))
        def _():
            right.wait_recv()

    position = lax.broadcasted_iota(jnp.int32, (1, wide), 1)
    column = position % row_len
    row = position // row_len - layers + s * rows + x * (rows // 2)
    inside = jnp.logical_and(row >= 0, row < rows * strips)
    diagonal = lax.broadcasted_iota(jnp.int32, (channels, channels), 0) == lax.broadcasted_iota(jnp.int32, (channels, channels), 1)

    def prepare(group):
        total = kernels[group, 0].astype(f32)
        for n in range(1, layers):
            total = total + kernels[group, n].astype(f32)
        summed = total[:, 0:channels]
        for t in range(1, taps):
            summed = summed + total[:, t * channels:(t + 1) * channels]
        return step_size * summed

    def turn(group):
        for n in range(layers):
            flipped = kernels[group, n].astype(f32)
            for t in range(taps):
                block = flipped[:, t * channels:(t + 1) * channels].T
                turned[group, n * channels:(n + 1) * channels, (taps - 1 - t) * channels:(taps - t) * channels] = block.astype(bf16)

    def evolve(group, matrix):
        current = window[group]
        value = current[:, edge:edge + half]
        mixed = exact_dot(exact_left(matrix), value)
        for n in range(layers):
            activation = jnp.where(inside, jnp.tanh(current), 0.0)
            own = activation[:, edge:edge + half]
            slopes[group, n] = 1.0 - own * own
            last = n == layers - 1
            first, count = (edge, half) if last else (0, wide)
            write_taps(stack, first, first, count, activation, column, row_len)
            forcing = jnp.dot(kernels[group, n], stack[:, first:first + count], preferred_element_type=f32)
            bias = jnp.sum(jnp.where(diagonal, biases[group, n:n + 1, :], 0.0), axis=1, keepdims=True)
            current = current[:, first:first + count] + step_size * (forcing + bias)
        offsets[group] = (current - value) - mixed

    for load in loads:
        load.wait()
    own_matrix = prepare(x)
    turn(x)
    wait_edge(x)
    evolve(x, own_matrix)

    arrivals = [
        remote(guess_in.at[0, 0, :, mine], window.at[other, :, place], swap_send.at[0], swap_recv.at[0], partner, s),
        remote(kernels_in, kernels.at[other], swap_send.at[1], swap_recv.at[1], partner, s),
        remote(biases_in, biases.at[other], swap_send.at[2], swap_recv.at[2], partner, s),
    ]
    for arrival in arrivals:
        arrival.wait_recv()
    other_matrix = prepare(other)
    wait_edge(other)
    evolve(other, other_matrix)

    early = jnp.where(even, own_matrix, other_matrix)
    late = jnp.where(even, other_matrix, own_matrix)
    late_left = exact_left(late)
    both = early + late + exact_dot(late_left, early)
    map_left = exact_left(jnp.concatenate([both, early], axis=0))
    early_off = offsets[0]
    sum_offs[...] = offsets[1] + early_off + exact_dot(late_left, early_off)

    trace_copies = [remote(trace_out, trace_in.at[d], trace_send.at[d], trace_recv.at[d], ring[d][0], ring[d][1])
                    for d in range(2 * strips - 1)]

    def strip_traces():
        left = remote(probes_in.at[:, 0, :, last_rows], probes.at[:, :, pl.ds(0, edge)], edge_send.at[2], edge_recv.at[2], k, s)
        right = remote(probes_in.at[:, 0, :, first_rows], probes.at[:, :, pl.ds(part, edge)], edge_send.at[2], edge_recv.at[2], k, s)

        @pl.when(jnp.logical_and(even, has_down))
        def _():
            left.wait_recv()

        @pl.when(jnp.logical_and(x == 1, has_up))
        def _():
            right.wait_recv()

        turn(other)
        sums = [jnp.zeros((8, LANES), f32) for _ in range(2 * layers)]
        for p in range(probe_count):
            padded = jnp.where(inside, probes[p].astype(f32), 0.0)
            field = padded[:, edge:edge + half]
            write_taps(probe_stack, 0, edge, half, padded, column, row_len)
            for group in range(2):
                weights = jnp.dot(turned[group], probe_stack[...], preferred_element_type=f32)
                for n in range(layers):
                    tangent = (slopes[group, n] * field).astype(bf16).astype(f32)
                    product = tangent * weights[n * channels:(n + 1) * channels]
                    folded = product[:, 0:LANES]
                    for c in range(1, chunks):
                        folded = folded + product[:, c * LANES:(c + 1) * LANES]
                    for r in range(channels // 8):
                        sums[group * layers + n] = sums[group * layers + n] + folded[r * 8:(r + 1) * 8]
        for i in range(2 * layers):
            trace_out[i * 8:(i + 1) * 8] = sums[i]
        for copy in trace_copies:
            copy.start()

    @pl.when(q > 0)
    def _():
        strip_traces()

    nexts = [remote(chain_out.at[c], chain_in.at[c], chain_send.at[c], chain_recv.at[c], k + 2, s) for c in range(chunks)]
    passes = [remote(pass_out.at[c], states.at[0, 0, :, chunk(x, c)], pass_send.at[c], pass_recv.at[c], partner, s)
              for c in range(chunks)]
    passed = [remote(pass_out.at[c], states.at[0, 0, :, chunk(1 - x, c)], pass_send.at[c], pass_recv.at[c], partner, s)
              for c in range(chunks)]
    onward = remote(run_out, run_in, run_sem.at[0], run_sem.at[1], k + 2, s)
    go_on = q < pairs - 1

    for c in range(chunks):
        piece = slice(c * LANES, (c + 1) * LANES)

        @pl.when(q == 0)
        def _():
            chain_in[c] = window[0, :, edge + c * LANES:edge + (c + 1) * LANES]

        @pl.when(q > 0)
        def _():
            nexts[c].wait_recv()

        here = chain_in[c]
        moved = exact_dot(map_left, here)
        chain_out[c] = here + (moved[0:channels] + sum_offs[:, piece])

        @pl.when(go_on)
        def _():
            nexts[c].start()

        between = here + (moved[channels:2 * channels] + offsets[0, :, piece])
        pass_out[c] = jnp.where(even, between, here)
        passes[c].start()
        states[0, 0, :, chunk(x, c)] = jnp.where(even, here, between)

    @pl.when(q == 0)
    def _():
        strip_traces()

    for copy in trace_copies:
        copy.wait_recv()
    total = trace_out[...]
    for d in range(2 * strips - 1):
        total = total + trace_in[d]
    group_sums = []
    for group in range(2):
        tile = total[group * layers * 8:(group * layers + 1) * 8]
        for n in range(1, layers):
            tile = tile + total[(group * layers + n) * 8:(group * layers + n + 1) * 8]
        group_sums.append(tile)

    @pl.when(q == 0)
    def _():
        run_in[...] = jnp.zeros_like(run_in)

    @pl.when(q > 0)
    def _():
        onward.wait_recv()

    running = run_in[...]
    run_out[...] = running + group_sums[0] + group_sums[1]

    @pl.when(go_on)
    def _():
        onward.start()

    running = running + jnp.where(even, 0.0, group_sums[0])
    for n in range(layers):
        low, high = n * 8, (layers + n) * 8
        running = running + jnp.where(even, total[low:low + 8], total[high:high + 8])
        logs[n * 8:(n + 1) * 8] = running * (-(step_size / row_len) / probe_count)

    for c in range(chunks):
        passed[c].wait_recv()
    for c in range(chunks):
        passes[c].wait_send()
    for copy in trace_copies:
        copy.wait_send()
    for copy in swaps:
        copy.wait_send()

    @pl.when(go_on)
    def _():
        for c in range(chunks):
            nexts[c].wait_send()
        onward.wait_send()

    @pl.when(has_up)
    def _():
        up.wait_send()

    @pl.when(has_down)
    def _():
        down.wait_send()

    @pl.when(send_probe_up)
    def _():
        probe_up.wait_send()

    @pl.when(send_probe_down)
    def _():
        probe_down.wait_send()


def finish(states_in, tiles, states, logs, sem):
    pieces = sem.shape[0]
    size = states_in.shape[2] // pieces
    copies = [pltpu.make_async_copy(states_in.at[:, :, pl.ds(i * size, size)], states.at[:, :, pl.ds(i * size, size)], sem.at[i])
              for i in range(pieces)]
    for copy in copies:
        copy.start()
    for n in range(logs.shape[0]):
        logs[n] = jnp.sum(tiles[n * 8:(n + 1) * 8])
    for copy in copies:
        copy.wait()


def solution(mesh):
    peers, strips = mesh.shape["tm"], mesh.shape["space"]

    def step(guess, kernels, biases, probes):
        channels, cells = guess.shape[2], guess.shape[3]
        layers = kernels.shape[0]
        probe_count = probes.shape[0]
        edge = layers * WIDTH
        half = cells // 2
        chunks = half // LANES
        depth = kernels.shape[2]
        dma = pltpu.SemaphoreType.DMA
        tile = (chunks, channels, LANES)
        states, tiles = pl.pallas_call(
            functools.partial(kernel, peers, strips),
            out_shape=(
                pltpu.VMEM(guess.shape, f32),
                pltpu.VMEM((layers * 8, LANES), f32),
            ),
            in_specs=[pl.BlockSpec(memory_space=pl.ANY)] * 4,
            out_specs=(pl.BlockSpec(memory_space=pltpu.VMEM), pl.BlockSpec(memory_space=pltpu.VMEM)),
            scratch_shapes=[
                pltpu.VMEM((2, channels, half + 2 * edge), f32),
                pltpu.VMEM((2,) + kernels.shape, kernels.dtype),
                pltpu.VMEM((2,) + biases.shape, biases.dtype),
                pltpu.VMEM((probe_count, channels, half + 2 * edge), bf16),
                pltpu.VMEM((depth, half + 2 * edge), bf16),
                pltpu.VMEM((depth, half), bf16),
                pltpu.VMEM((2, layers * channels, depth), bf16),
                pltpu.VMEM((2, channels, half), f32),
                pltpu.VMEM((2, layers, channels, half), f32),
                pltpu.VMEM((channels, half), f32),
                pltpu.VMEM(tile, f32),
                pltpu.VMEM(tile, f32),
                pltpu.VMEM(tile, f32),
                pltpu.VMEM((2 * layers * 8, LANES), f32),
                pltpu.VMEM((2 * strips - 1, 2 * layers * 8, LANES), f32),
                pltpu.VMEM((8, LANES), f32),
                pltpu.VMEM((8, LANES), f32),
                dma((4,)), dma((3,)), dma((3,)), dma((3,)), dma((3,)), dma((chunks,)), dma((chunks,)),
                dma((chunks,)), dma((chunks,)), dma((2 * strips - 1,)), dma((2 * strips - 1,)), dma((2,)),
            ],
            compiler_params=pltpu.CompilerParams(collective_id=0, has_side_effects=True),
        )(guess, kernels, biases, probes)
        return pl.pallas_call(
            finish,
            out_shape=(
                jax.ShapeDtypeStruct(guess.shape, f32),
                jax.ShapeDtypeStruct((layers,), f32),
            ),
            in_specs=[pl.BlockSpec(memory_space=pltpu.VMEM)] * 2,
            out_specs=(pl.BlockSpec(memory_space=pl.ANY), pl.BlockSpec(memory_space=pltpu.SMEM)),
            scratch_shapes=[dma((4,))],
        )(pltpu.with_memory_space_constraint(states, pltpu.VMEM), pltpu.with_memory_space_constraint(tiles, pltpu.VMEM))

    return jax.shard_map(
        step,
        mesh=mesh,
        in_specs=(
            P("tm", None, None, "space"),
            P("tm", None, None),
            P("tm", None),
            P(None, None, None, "space"),
        ),
        out_specs=(P("tm", None, None, "space"), P("tm")),
        check_vma=False,
    )
```

```python
import functools

import jax
import jax.numpy as jnp
from jax import lax
from jax.experimental import pallas as pl
from jax.experimental.pallas import tpu as pltpu
from jax.sharding import PartitionSpec as P

WIDTH = 64
LANES = 128
MESH = pl.DeviceIdType.MESH
step_size = 0.0078125
f32 = jnp.float32
bf16 = jnp.bfloat16


def split(value):
    high = value.astype(bf16)
    low = (value - high.astype(f32)).astype(bf16)
    return high, low


def exact_left(matrix):
    high, low = split(matrix)
    return jnp.concatenate([high.astype(f32), high.astype(f32), low.astype(f32)], axis=1).astype(bf16)


def exact_dot(left, field):
    high, low = split(field)
    return jnp.dot(left, jnp.concatenate([high, low, high], axis=0), preferred_element_type=f32)


def write_taps(target, base, first, count, value, column, row_len):
    width = value.shape[1]
    left = jnp.where(column != 0, pltpu.roll(value, 1, 1), 0.0)
    right = jnp.where(column != row_len - 1, pltpu.roll(value, width - 1, 1), 0.0)
    channels = value.shape[0]
    for dy in (-1, 0, 1):
        for index, source in enumerate((left, value, right)):
            tap = (dy + 1) * 3 + index
            moved = source if dy == 0 else pltpu.roll(source, (-dy * row_len) % width, 1)
            target[tap * channels:(tap + 1) * channels, base:base + count] = moved[:, first:first + count].astype(bf16)


def kernel(peers, strips, guess_in, kernels_in, biases_in, probes_in, states, logs,
           guess, kernels, biases, probes, load_sem, halo, probe_halo, stack, probe_stack, turned, mine, theirs, own_out, their_off, early_offs, sum_offs,
           chain_in, chain_out, pass_out, trace_out, trace_in, pair_out, pair_in, run_out, run_in,
           halo_send, halo_recv, mat_sem, off_send, off_recv, chain_send, chain_recv,
           pass_send, pass_recv, trace_send, trace_recv, small_sem):
    row_len = WIDTH
    channels, cells = guess.shape[2], guess.shape[3]
    layers = kernels.shape[0]
    probe_count = probes.shape[0]
    taps = 9
    edge = layers * row_len
    wide = cells + 2 * edge
    rows = cells // row_len
    half = cells // 2
    chunks = half // LANES
    k = lax.axis_index("tm")
    s = lax.axis_index("space")
    q, x = k // 2, k % 2
    partner = q * 2 + 1 - x
    pairs = peers // 2

    def remote(src, dst, send, recv, tm, space):
        return pltpu.make_async_remote_copy(
            src_ref=src, dst_ref=dst, send_sem=send, recv_sem=recv, device_id=(tm, space), device_id_type=MESH)

    def chunk(side, c):
        return pl.ds(pl.multiple_of(side * half + c * LANES, LANES), LANES)

    loads = [pltpu.make_async_copy(src, dst, load_sem.at[i]) for i, (src, dst) in enumerate(
        ((kernels_in, kernels), (guess_in, guess), (biases_in, biases), (probes_in, probes)))]
    for load in loads:
        load.start()

    barrier = pltpu.get_barrier_semaphore()
    for d in range(1, strips):
        pl.semaphore_signal(barrier, inc=1, device_id=(k, lax.rem(s + d, strips)), device_id_type=MESH)
    pl.semaphore_signal(barrier, inc=1, device_id=(partner, s), device_id_type=MESH)

    @pl.when(q > 0)
    def _():
        pl.semaphore_signal(barrier, inc=1, device_id=(k - 2, s), device_id_type=MESH)

    @pl.when(q < pairs - 1)
    def _():
        pl.semaphore_signal(barrier, inc=1, device_id=(k + 2, s), device_id_type=MESH)

    pl.semaphore_wait(barrier, strips + (q > 0).astype(jnp.int32) + (q < pairs - 1).astype(jnp.int32))

    up = remote(guess_in.at[0, 0, :, pl.ds(cells - edge, edge)], halo.at[0], halo_send.at[0], halo_recv.at[0], k, s + 1)
    down = remote(guess_in.at[0, 0, :, pl.ds(0, edge)], halo.at[1], halo_send.at[1], halo_recv.at[1], k, s - 1)
    probe_up = remote(probes_in.at[:, 0, :, pl.ds(cells - edge, edge)], probe_halo.at[0], halo_send.at[2], halo_recv.at[2], k, s + 1)
    probe_down = remote(probes_in.at[:, 0, :, pl.ds(0, edge)], probe_halo.at[1], halo_send.at[3], halo_recv.at[3], k, s - 1)
    has_up, has_down = s < strips - 1, s > 0

    odd = s % 2 == 1

    @pl.when(jnp.logical_and(has_up, odd))
    def _():
        up.start()

    @pl.when(has_down)
    def _():
        down.start()

    @pl.when(jnp.logical_and(has_up, jnp.logical_not(odd)))
    def _():
        up.start()

    @pl.when(has_up)
    def _():
        probe_up.start()

    @pl.when(has_down)
    def _():
        probe_down.start()

    first_pair = jnp.logical_and(q == 0, x == 0)
    seeds = [remote(guess_in.at[0, 0, :, pl.ds(half + c * LANES, LANES)], chain_in.at[c], pass_send.at[chunks + c], chain_recv.at[c], partner, s)
             for c in range(chunks)]

    @pl.when(first_pair)
    def _():
        for c in range(chunks):
            seeds[c].start()

    for load in loads:
        load.wait()

    @pl.when(first_pair)
    def _():
        for c in range(chunks):
            chain_in[c] = guess[0, 0, :, c * LANES:(c + 1) * LANES]

    total = kernels[0].astype(f32)
    for n in range(1, layers):
        total = total + kernels[n].astype(f32)
    summed = total[:, 0:channels]
    for t in range(1, taps):
        summed = summed + total[:, t * channels:(t + 1) * channels]
    own_matrix = step_size * summed
    mine[:, 0:channels] = own_matrix
    mine[:, channels:2 * channels] = own_matrix
    mat = remote(mine, theirs, mat_sem.at[0], mat_sem.at[1], partner, s)
    mat.start()

    for n in range(layers):
        flipped = kernels[n].astype(f32)
        for t in range(taps):
            block = flipped[:, t * channels:(t + 1) * channels].T
            turned[n * channels:(n + 1) * channels, (taps - 1 - t) * channels:(taps - t) * channels] = block.astype(bf16)

    value = guess[0, 0]
    own_left = exact_left(own_matrix)
    mixed = exact_dot(own_left, value)

    position = lax.broadcasted_iota(jnp.int32, (1, wide), 1)
    column = position % row_len
    row = position // row_len - layers + s * rows
    inside = jnp.logical_and(row >= 0, row < rows * strips)
    diagonal = lax.broadcasted_iota(jnp.int32, (channels, channels), 0) == lax.broadcasted_iota(jnp.int32, (channels, channels), 1)

    @pl.when(has_down)
    def _():
        up.wait_recv()

    @pl.when(has_up)
    def _():
        down.wait_recv()

    current = jnp.concatenate([halo[0], value, halo[1]], axis=1)
    slopes = []
    for n in range(layers):
        activation = jnp.where(inside, jnp.tanh(current), 0.0)
        own = activation[:, edge:edge + cells]
        slopes.append(1.0 - own * own)
        last = n == layers - 1
        first, count = (edge, cells) if last else (0, wide)
        write_taps(stack, first, first, count, activation, column, row_len)
        forcing = jnp.dot(kernels[n], stack[:, first:first + count], preferred_element_type=f32)
        bias = jnp.sum(jnp.where(diagonal, biases[n:n + 1, :], 0.0), axis=1, keepdims=True)
        current = current[:, first:first + count] + step_size * (forcing + bias)
    own_out[...] = (current - value) - mixed

    offs = [remote(own_out.at[:, chunk(1 - x, c)], their_off.at[c], off_send.at[c], off_recv.at[c], partner, s)
            for c in range(chunks)]
    for c in range(chunks):
        offs[c].start()

    @pl.when(has_down)
    def _():
        probe_up.wait_recv()

    @pl.when(has_up)
    def _():
        probe_down.wait_recv()

    sums = [jnp.zeros((8, LANES), f32) for _ in range(layers)]
    for p in range(probe_count):
        field = probes[p, 0].astype(f32)
        padded = jnp.concatenate([probe_halo[0, p].astype(f32), field, probe_halo[1, p].astype(f32)], axis=1)
        padded = jnp.where(inside, padded, 0.0)
        write_taps(probe_stack, 0, edge, cells, padded, column, row_len)
        weights = jnp.dot(turned[...], probe_stack[...], preferred_element_type=f32)
        for n in range(layers):
            tangent = (slopes[n] * field).astype(bf16).astype(f32)
            product = tangent * weights[n * channels:(n + 1) * channels]
            part = product[:, 0:LANES]
            for c in range(1, cells // LANES):
                part = part + product[:, c * LANES:(c + 1) * LANES]
            for r in range(channels // 8):
                sums[n] = sums[n] + part[r * 8:(r + 1) * 8]
    for n in range(layers):
        trace_out[n * 8:(n + 1) * 8] = sums[n]
    traces = [remote(trace_out, trace_in.at[d - 1], trace_send.at[d - 1], trace_recv.at[d - 1], k, lax.rem(s + d, strips))
              for d in range(1, strips)]
    for copy in traces:
        copy.start()

    mat.wait_recv()
    other_matrix = theirs[:, 0:channels]
    even = x == 0
    early = jnp.where(even, own_matrix, other_matrix)
    late = jnp.where(even, other_matrix, own_matrix)
    late_left = exact_left(late)
    both = early + late + exact_dot(late_left, early)
    map_left = exact_left(jnp.concatenate([both, early], axis=0))

    nexts = [remote(chain_out.at[c], chain_in.at[c], chain_send.at[c], chain_recv.at[c], k + 2, s) for c in range(chunks)]
    passes = [remote(pass_out.at[c], states.at[0, 0, :, chunk(x, c)], pass_send.at[c], pass_recv.at[c], partner, s)
              for c in range(chunks)]
    relays = [remote(chain_in.at[c], states.at[0, 0, :, chunk(x, c)], pass_send.at[c], pass_recv.at[c], partner, s)
              for c in range(chunks)]
    passed = [remote(pass_out.at[c], states.at[0, 0, :, chunk(1 - x, c)], pass_send.at[c], pass_recv.at[c], partner, s)
              for c in range(chunks)]
    pair = remote(pair_out, pair_in, small_sem.at[0], small_sem.at[1], partner, s)
    onward = remote(run_out, run_in, small_sem.at[2], small_sem.at[3], k + 2, s)
    go_on = q < pairs - 1
    waits = jnp.logical_not(first_pair)
    def prepare(c):
        offs[c].wait_recv()
        held = own_out[:, chunk(x, c)]
        got = their_off[c]
        early_off = jnp.where(even, held, got)
        late_off = jnp.where(even, got, held)
        early_offs[c] = early_off
        sum_offs[c] = late_off + early_off + exact_dot(late_left, early_off)

    def strip_traces():
        trace_total = trace_out[...]
        for copy in traces:
            copy.wait_recv()
        for d in range(1, strips):
            trace_total = trace_total + trace_in[d - 1]
        pair_out[...] = trace_total
        pair.start()

    @pl.when(q > 0)
    def _():
        for c in range(chunks):
            prepare(c)
        strip_traces()

    for c in range(chunks):
        @pl.when(q == 0)
        def _():
            prepare(c)

        @pl.when(waits)
        def _():
            nexts[c].wait_recv()

        @pl.when(x == 1)
        def _():
            relays[c].start()

        here = chain_in[c]
        moved = exact_dot(map_left, here)
        chain_out[c] = here + (moved[0:channels] + sum_offs[c])

        @pl.when(go_on)
        def _():
            nexts[c].start()

        between = here + (moved[channels:2 * channels] + early_offs[c])
        pass_out[c] = between

        @pl.when(even)
        def _():
            passes[c].start()

        states[0, 0, :, chunk(x, c)] = jnp.where(even, here, between)
        if c == max(chunks - 2, 0):
            @pl.when(q == 0)
            def _():
                strip_traces()

    pair.wait_recv()

    trace_total = pair_out[...]

    def layer_sum(tile):
        result = tile[0:8]
        for n in range(1, layers):
            result = result + tile[n * 8:(n + 1) * 8]
        return result

    own_sum, pair_sum = layer_sum(trace_total), layer_sum(pair_in[...])

    @pl.when(q == 0)
    def _():
        run_in[...] = jnp.zeros_like(run_in)

    @pl.when(q > 0)
    def _():
        onward.wait_recv()

    running = run_in[...]
    run_out[...] = running + own_sum + pair_sum

    @pl.when(go_on)
    def _():
        onward.start()

    running = running + jnp.where(even, 0.0, pair_sum)
    for n in range(layers):
        running = running + trace_total[n * 8:(n + 1) * 8]
        logs[n * 8:(n + 1) * 8] = running * (-(step_size / row_len) / probe_count)

    for c in range(chunks):
        passed[c].wait_recv()
    for c in range(chunks):
        passes[c].wait_send()
        offs[c].wait_send()
    for copy in traces:
        copy.wait_send()
    mat.wait_send()
    pair.wait_send()

    @pl.when(go_on)
    def _():
        for c in range(chunks):
            nexts[c].wait_send()
        onward.wait_send()

    @pl.when(first_pair)
    def _():
        for c in range(chunks):
            seeds[c].wait_send()

    @pl.when(has_up)
    def _():
        up.wait_send()
        probe_up.wait_send()

    @pl.when(has_down)
    def _():
        down.wait_send()
        probe_down.wait_send()


def finish(states_in, tiles, states, logs, sem):
    pieces = sem.shape[0]
    size = states_in.shape[2] // pieces
    copies = [pltpu.make_async_copy(states_in.at[:, :, pl.ds(i * size, size)], states.at[:, :, pl.ds(i * size, size)], sem.at[i])
              for i in range(pieces)]
    for copy in copies:
        copy.start()
    for n in range(logs.shape[0]):
        logs[n] = jnp.sum(tiles[n * 8:(n + 1) * 8])
    for copy in copies:
        copy.wait()


def solution(mesh):
    peers, strips = mesh.shape["tm"], mesh.shape["space"]

    def step(guess, kernels, biases, probes):
        channels, cells = guess.shape[2], guess.shape[3]
        layers = kernels.shape[0]
        probe_count = probes.shape[0]
        edge = layers * WIDTH
        chunks = cells // 2 // LANES
        depth = kernels.shape[2]
        dma = pltpu.SemaphoreType.DMA
        tile = (chunks, channels, LANES)
        states, tiles = pl.pallas_call(
            functools.partial(kernel, peers, strips),
            out_shape=(
                pltpu.VMEM(guess.shape, f32),
                pltpu.VMEM((layers * 8, LANES), f32),
            ),
            in_specs=[pl.BlockSpec(memory_space=pl.ANY)] * 4,
            out_specs=(pl.BlockSpec(memory_space=pltpu.VMEM), pl.BlockSpec(memory_space=pltpu.VMEM)),
            scratch_shapes=[
                pltpu.VMEM(guess.shape, guess.dtype),
                pltpu.VMEM(kernels.shape, kernels.dtype),
                pltpu.VMEM(biases.shape, biases.dtype),
                pltpu.VMEM(probes.shape, probes.dtype),
                dma((4,)),
                pltpu.VMEM((2, channels, edge), f32),
                pltpu.VMEM((2, probe_count, channels, edge), bf16),
                pltpu.VMEM((depth, cells + 2 * edge), bf16),
                pltpu.VMEM((depth, cells), bf16),
                pltpu.VMEM((layers * channels, depth), bf16),
                pltpu.VMEM((channels, 2 * channels), f32),
                pltpu.VMEM((channels, 2 * channels), f32),
                pltpu.VMEM((channels, cells), f32),
                pltpu.VMEM(tile, f32),
                pltpu.VMEM(tile, f32),
                pltpu.VMEM(tile, f32),
                pltpu.VMEM(tile, f32),
                pltpu.VMEM(tile, f32),
                pltpu.VMEM(tile, f32),
                pltpu.VMEM((layers * 8, LANES), f32),
                pltpu.VMEM((max(strips - 1, 1), layers * 8, LANES), f32),
                pltpu.VMEM((layers * 8, LANES), f32),
                pltpu.VMEM((layers * 8, LANES), f32),
                pltpu.VMEM((8, LANES), f32),
                pltpu.VMEM((8, LANES), f32),
                dma((4,)), dma((4,)), dma((2,)), dma((chunks,)), dma((chunks,)), dma((chunks,)), dma((chunks,)),
                dma((2 * chunks,)), dma((chunks,)), dma((max(strips - 1, 1),)), dma((max(strips - 1, 1),)), dma((4,)),
            ],
            compiler_params=pltpu.CompilerParams(collective_id=0, has_side_effects=True),
        )(guess, kernels, biases, probes)
        return pl.pallas_call(
            finish,
            out_shape=(
                jax.ShapeDtypeStruct(guess.shape, f32),
                jax.ShapeDtypeStruct((layers,), f32),
            ),
            in_specs=[pl.BlockSpec(memory_space=pltpu.VMEM)] * 2,
            out_specs=(pl.BlockSpec(memory_space=pl.ANY), pl.BlockSpec(memory_space=pltpu.SMEM)),
            scratch_shapes=[dma((4,))],
        )(pltpu.with_memory_space_constraint(states, pltpu.VMEM), pltpu.with_memory_space_constraint(tiles, pltpu.VMEM))

    return jax.shard_map(
        step,
        mesh=mesh,
        in_specs=(
            P("tm", None, None, "space"),
            P("tm", None, None),
            P("tm", None),
            P(None, None, None, "space"),
        ),
        out_specs=(P("tm", None, None, "space"), P("tm")),
        check_vma=False,
    )
```
